32 devices in a mesh: dp: 2 (over x), space: 16 (over z, y, core).
Axes of the slice: x: 2, y: 2, z: 4, core: 2. Of those that a mesh axis runs over, the one named last changes fastest.
Arguments:
- stash: bfloat16 [16, 16, 4, 8640], P('space', None, 'dp'), may hold values from -5 to 5
- piece_map: int32 [16, 16], P(None, 'space'), may hold values from 0 to 15, as said below
- gain_one: float32 [768], replicated, may hold values from 0.5 to 1.5
- spec_one: float32 [2, 8, 96, 96], replicated, may hold values from -0.4375 to 0.4375
- bias_one: float32 [2, 768], replicated, may hold values from -3 to 3
- spec_two: float32 [2, 8, 96, 96], replicated, may hold values from -0.4375 to 0.4375
- bias_two: float32 [2, 768], replicated, may hold values from -0.6 to 0.6
- gain_two: float32 [768], replicated, may hold values from 0.5 to 1.5
- fc_one: bfloat16 [768, 3072], replicated, may hold values from -0.21875 to 0.21875
- bias_fc: float32 [3072], replicated, may hold values from -3 to 3
- fc_two: bfloat16 [3072, 768], replicated, may hold values from -0.109375 to 0.109375
- cotangent: bfloat16 [4, 16, 180, 768], P('dp', 'space'), may hold values from -6 to 6
Outputs:
- grad_input: float32 [4, 16, 180, 768], P('dp', 'space')
- grad_fc_one: float32 [768, 3072], P(None, ('dp', 'space'))
- grad_fc_two: float32 [3072, 768], P(('dp', 'space'))
- grad_bias_fc: float32 [3072], replicated
- grad_bias_out: float32 [768], replicated
- grad_gain_one: float32 [768], replicated
- grad_gain_two: float32 [768], replicated
- grad_spec_one: float32 [2, 8, 96, 96], replicated
- grad_bias_one: float32 [2, 768], replicated
- grad_spec_two: float32 [2, 8, 96, 96], replicated
- grad_bias_two: float32 [2, 768], replicated
The draws below stay inside these ranges and needn't reach their ends.
Inputs may be any that keep to these rules, and one draw needn't show every extreme that they name: `piece_map`: each column holds every number from 0 to 15 once.
All inputs are finite; a program needn't handle non-finite values.
Results may differ from the reference program's by a relative error of at most 0.0046.
Values may be sent and summed in bfloat16 or wider, within the bound.
A program may use at most 128 MiB of HBM per device.

```python
import jax
import jax.numpy as jnp
from jax import lax

D = 768
FF = 3072
BLOCKS = 8
LON = 180
KW = 64
BLOCK = 96
H = 16
SAMPLES = 4
PIECE = 8640
N_SPACE = 16


def piece_table(key):

    def one_column(column):
        return jax.random.permutation(jax.random.fold_in(key, column), N_SPACE)
    columns = jax.vmap(one_column)(jnp.arange(N_SPACE, dtype=jnp.int32))
    return columns.T.astype(jnp.int32)


def draw_piece_map(key, part):
    return piece_table(jax.random.fold_in(key, 11))


def draw_stash(key, part):
    holder_table = piece_table(jax.random.fold_in(key, 11))
    drawn_field = jnp.clip(jax.random.normal(jax.random.fold_in(key, 29), (SAMPLES, H, LON, D), jnp.float32), -5.0, 5.0)
    pieces = drawn_field.reshape(SAMPLES, N_SPACE, N_SPACE, PIECE)
    pieces = jnp.transpose(pieces, (1, 2, 0, 3))
    owners = jnp.arange(N_SPACE, dtype=jnp.int32)[None, :]
    return pieces[owners, holder_table].astype(jnp.bfloat16)


def block_levels(key, extent, cuts, low, largest):
    loudness, own = 1.0, jax.random.fold_in(key, 6)
    for axis_at, shards_of in cuts:
        steps = jnp.exp(jax.random.uniform(jax.random.fold_in(own, axis_at), (shards_of,), jnp.float32, low / len(cuts), largest / len(cuts)))
        loudness = loudness * jnp.repeat(steps, extent[axis_at] // shards_of).reshape([-1 if axis == axis_at else 1 for axis in range(len(extent))])
    return loudness


def scatter_about(rng, dims, scale, limit, split=(), held_as=jnp.bfloat16):
    drawn = scale * jax.random.normal(rng, dims, jnp.float32)
    if split:
        drawn = drawn * block_levels(rng, dims, split, -0.22, 0.18)
    return jnp.clip(drawn, -limit, limit).astype(held_as)


def setup_inputs(seed: int = 0) -> dict:
    key_of = jax.random.split(jax.random.key(seed), 13)
    return {
        "stash": draw_stash(jax.random.fold_in(key_of[12], 71), 0),
        "piece_map": draw_piece_map(jax.random.fold_in(key_of[12], 71), 0),
        "gain_one": jnp.clip(1.0 + 0.1 * jax.random.normal(key_of[2], (D,), jnp.float32), 0.5, 1.5),
        "spec_one": scatter_about(key_of[3], (2, BLOCKS, BLOCK, BLOCK), (2 * BLOCK) ** -0.5, 0.4375, (), jnp.float32),
        "bias_one": scatter_about(key_of[4], (2, D), 0.5, 3.0, (), jnp.float32),
        "spec_two": scatter_about(key_of[5], (2, BLOCKS, BLOCK, BLOCK), (2 * BLOCK) ** -0.5, 0.4375, (), jnp.float32),
        "bias_two": scatter_about(key_of[6], (2, D), 0.1, 0.6, (), jnp.float32),
        "gain_two": jnp.clip(1.0 + 0.1 * jax.random.normal(key_of[7], (D,), jnp.float32), 0.5, 1.5),
        "fc_one": scatter_about(key_of[8], (D, FF), D ** -0.5, 0.21875),
        "bias_fc": scatter_about(key_of[9], (FF,), 0.5, 3.0, (), jnp.float32),
        "fc_two": scatter_about(key_of[10], (FF, D), FF ** -0.5, 0.109375),
        "cotangent": scatter_about(key_of[11], (SAMPLES, H, LON, D), 1.0, 6.0, ((0, 2), (1, 16))),
    }


epsilon = 1e-05
highest = lax.Precision.HIGHEST

def layer_norm(values, gain_vector):
    centred = values - lax.optimization_barrier(jnp.mean(values, axis=-1, keepdims=True))
    spread = lax.optimization_barrier(jnp.mean(centred * centred, axis=-1, keepdims=True))
    return centred * lax.rsqrt(spread + epsilon) * gain_vector

def smooth_gate(values):
    return jax.nn.gelu(values, approximate=True)

def block_mix(real_part, imag_part, weights, biases):
    blocks = weights.shape[1]
    width_block = weights.shape[2]
    leading = real_part.shape[:-1]
    real_blocks = real_part.reshape(leading + (blocks, width_block))
    imag_blocks = imag_part.reshape(leading + (blocks, width_block))
    bias_real = biases[0].reshape(blocks, width_block)
    bias_imag = biases[1].reshape(blocks, width_block)
    new_real = jnp.einsum('...ni,nio->...no', real_blocks, weights[0], precision=highest) - jnp.einsum('...ni,nio->...no', imag_blocks, weights[1], precision=highest) + bias_real
    new_imag = jnp.einsum('...ni,nio->...no', real_blocks, weights[1], precision=highest) + jnp.einsum('...ni,nio->...no', imag_blocks, weights[0], precision=highest) + bias_imag
    return (new_real.reshape(leading + (blocks * width_block,)), new_imag.reshape(leading + (blocks * width_block,)))

def spectral_mlp(spec_real, spec_imag, spec_one, bias_one, spec_two, bias_two):
    inner_real, inner_imag = block_mix(spec_real, spec_imag, spec_one, bias_one)
    return block_mix(smooth_gate(inner_real), smooth_gate(inner_imag), spec_two, bias_two)

def to_spectrum(normed):
    full = jnp.fft.rfft2(normed, axes=(0, 1), norm='ortho')[:, :KW, :]
    return (jnp.real(full), jnp.imag(full))

def from_spectrum(real_part, imag_part):
    spectrum = lax.complex(real_part, imag_part)
    padded = jnp.pad(spectrum, ((0, 0), (0, LON // 2 + 1 - KW), (0, 0)))
    return jnp.fft.irfft2(padded, s=(H, LON), axes=(0, 1), norm='ortho')

def reference(stash, piece_map, gain_one, spec_one, bias_one, spec_two, bias_two, gain_two, fc_one, bias_fc, fc_two, cotangent):
    holders = jnp.argsort(piece_map, axis=0).astype(jnp.int32)
    owners = jnp.arange(N_SPACE, dtype=jnp.int32)[None, :]
    gathered = stash[holders, owners]
    inputs = jnp.transpose(gathered, (2, 1, 0, 3)).reshape(SAMPLES, H, LON, D)

    def per_sample(carry, pair):
        sample_input, sample_cot = pair
        base_field = sample_input.astype(jnp.float32)
        normed, pull_one = jax.vjp(layer_norm, base_field, gain_one)
        spectrum, pull_spectrum = jax.vjp(to_spectrum, normed)
        mixed_spec, pull_mix = jax.vjp(spectral_mlp, spectrum[0], spectrum[1], spec_one, bias_one, spec_two, bias_two)
        spatial, pull_back = jax.vjp(from_spectrum, mixed_spec[0], mixed_spec[1])
        mixed_field = base_field + normed + spatial
        normed_two, pull_two = jax.vjp(layer_norm, mixed_field, gain_two)
        normed_flat = normed_two.astype(jnp.bfloat16).reshape(H * LON, D)
        hidden_pre = jnp.dot(normed_flat, fc_one, preferred_element_type=jnp.float32) + bias_fc
        active, pull_gate = jax.vjp(smooth_gate, hidden_pre)
        active_flat = active.astype(jnp.bfloat16)
        upstream = sample_cot.reshape(H * LON, D)
        grad_active = jnp.dot(upstream, fc_two.T, preferred_element_type=jnp.float32)
        grad_hidden = pull_gate(grad_active)[0]
        grad_hidden_flat = grad_hidden.astype(jnp.bfloat16)
        grad_normed_two = jnp.dot(grad_hidden_flat, fc_one.T, preferred_element_type=jnp.float32)
        term_one = jnp.dot(normed_flat.T, grad_hidden_flat, preferred_element_type=jnp.float32)
        term_two = jnp.dot(upstream.T, active_flat, preferred_element_type=jnp.float32)
        grad_mixed_norm, grad_gain_two = pull_two(grad_normed_two.reshape(H, LON, D))
        grad_mixed = sample_cot.astype(jnp.float32) + grad_mixed_norm
        grad_spectral = pull_back(grad_mixed)
        pulled = pull_mix(grad_spectral)
        grad_normed = grad_mixed + pull_spectrum((pulled[0], pulled[1]))[0]
        grad_base, grad_gain_one = pull_one(grad_normed)
        grad_sample = grad_mixed + grad_base
        bias_sum = lax.optimization_barrier(jnp.sum(grad_hidden, axis=0))
        out_sum = lax.optimization_barrier(jnp.sum(sample_cot.astype(jnp.float32), axis=(0, 1)))
        updates = (term_one, term_two, bias_sum, out_sum, grad_gain_one, grad_gain_two, pulled[2], pulled[3], pulled[4], pulled[5])
        carry = tuple((old + new for old, new in zip(carry, updates)))
        return (carry, grad_sample)
    start = (jnp.zeros((D, FF), jnp.float32), jnp.zeros((D, FF), jnp.float32), jnp.zeros((FF,), jnp.float32), jnp.zeros((D,), jnp.float32), jnp.zeros((D,), jnp.float32), jnp.zeros((D,), jnp.float32), jnp.zeros((2, BLOCKS, BLOCK, BLOCK), jnp.float32), jnp.zeros((2, D), jnp.float32), jnp.zeros((2, BLOCKS, BLOCK, BLOCK), jnp.float32), jnp.zeros((2, D), jnp.float32))
    sums, grad_input = lax.scan(per_sample, start, (inputs, cotangent))
    grad_scale = 1.0 / float(SAMPLES * H * LON) ** 0.5
    return (grad_input, sums[0] * grad_scale, sums[1].T * grad_scale, sums[2] * grad_scale, sums[3] * grad_scale, sums[4] * grad_scale, sums[5] * grad_scale, sums[6] * grad_scale, sums[7] * grad_scale, sums[8] * grad_scale, sums[9] * grad_scale)
```

```python
import math

import jax
import jax.numpy as jnp
import numpy as np
from jax import lax
from jax.sharding import PartitionSpec as P

KW = 64


epsilon = 1e-05
high = lax.Precision.HIGH
everyone = ("dp", "space")


def layer_norm(values, gain_vector):
    centred = values - jnp.mean(values, axis=-1, keepdims=True)
    spread = jnp.mean(centred * centred, axis=-1, keepdims=True)
    return centred * lax.rsqrt(spread + epsilon) * gain_vector


def smooth_gate(values):
    return jax.nn.gelu(values, approximate=True)


def complex_blocks(weights):
    top = jnp.concatenate((weights[0], weights[1]), axis=2)
    bottom = jnp.concatenate((-weights[1], weights[0]), axis=2)
    return jnp.concatenate((top, bottom), axis=1)


def complex_bias(biases, blocks):
    return biases.reshape(2, blocks, 1, -1).transpose(1, 2, 0, 3).reshape(blocks, 1, -1)


def block_dot(values, weights):
    return jnp.einsum("nri,nio->nro", values, weights, precision=high)


def spectral_mlp(spectrum, spec_one, bias_one, spec_two, bias_two):
    blocks = spec_one.shape[1]
    inner = block_dot(spectrum, complex_blocks(spec_one)) + complex_bias(bias_one, blocks)
    return block_dot(smooth_gate(inner), complex_blocks(spec_two)) + complex_bias(bias_two, blocks)


def zonal_tables(length, ranks):
    positions = np.arange(length)[:, None]
    frequency = np.arange(KW)[None, :]
    angles = (positions * frequency % length) * (2.0 * math.pi / length)
    table = np.stack((np.cos(angles), -np.sin(angles))) / math.sqrt(length)
    doubled = table * np.where(frequency == 0, 1.0, 2.0)
    shaped = [
        item.reshape(2, length, ranks, KW // ranks).transpose(1, 2, 0, 3).astype(np.float32)
        for item in (table, doubled)
    ]
    return shaped


def meridian_table(length, ranks):
    positions = np.arange(length)
    angles = (positions[:, None] * positions[None, :] % length) * (2.0 * math.pi / length)
    cosine = np.cos(angles) / math.sqrt(length)
    sine = np.sin(angles) / math.sqrt(length)
    table = np.stack((np.stack((cosine, -sine), -1), np.stack((sine, cosine), -1)), 1)
    return table.reshape(ranks, length // ranks, 2, length, 2).astype(np.float32)


def swap(pieces):
    return lax.all_to_all(pieces, "space", split_axis=0, concat_axis=0, tiled=True)


def to_modes(field, zonal, merid, blocks, carried):
    pieces = jnp.einsum("brwd,wscm->sbrcmd", field, zonal, precision=high)
    modes = swap(pieces.astype(carried)).astype(jnp.float32)
    spectrum = jnp.einsum("lbrcmd,lrcke->bmked", modes, merid, precision=high)
    rows = math.prod(spectrum.shape[:3])
    split = spectrum.reshape(rows, 2, blocks, -1)
    return split.transpose(2, 0, 1, 3).reshape(blocks, rows, -1)


def from_modes(spectrum, zonal, merid, samples, width, carried):
    blocks, rows = spectrum.shape[:2]
    length = merid.shape[3]
    split = spectrum.reshape(blocks, rows, 2, -1).transpose(1, 2, 0, 3)
    shaped = split.reshape(samples, rows // (samples * length), length, 2, width)
    pieces = jnp.einsum("bmked,lrcke->lbrcmd", shaped, merid, precision=high)
    modes = swap(pieces.astype(carried)).astype(jnp.float32)
    return jnp.einsum("sbrcmd,wscm->brwd", modes, zonal, precision=high)


def local(
    stash,
    piece_map,
    gain_one,
    spec_one,
    bias_one,
    spec_two,
    bias_two,
    gain_two,
    fc_one,
    bias_fc,
    fc_two,
    cotangent,
):
    samples, lat_rows, lon_cells, model_width = cotangent.shape
    space_ranks = lax.axis_size("space")
    lat_total = lat_rows * space_ranks
    tokens = samples * lat_rows * lon_cells
    blocks = spec_one.shape[1]
    arrived = lax.all_to_all(stash, "space", split_axis=1, concat_axis=0, tiled=True)
    ordering = jnp.argsort(piece_map[:, 0])
    placed = jnp.take(arrived[:, 0], ordering, axis=0)
    inputs = jnp.transpose(placed, (1, 0, 2)).reshape(samples, lat_rows, lon_cells, model_width)
    base_field = inputs.astype(jnp.float32)
    zonal, zonal_back = zonal_tables(lon_cells, space_ranks)
    merid = meridian_table(lat_total, space_ranks)
    normed, pull_one = jax.vjp(layer_norm, base_field, gain_one)
    spectrum = to_modes(normed, zonal, merid, blocks, jnp.float32)
    mixed_spec, pull_mix = jax.vjp(spectral_mlp, spectrum, spec_one, bias_one, spec_two, bias_two)
    spatial = from_modes(
        mixed_spec, zonal_back, merid, samples, model_width, jnp.float32
    )
    mixed_field = base_field + normed + spatial
    normed_two, pull_two = jax.vjp(layer_norm, mixed_field, gain_two)
    normed_flat = normed_two.astype(jnp.bfloat16).reshape(tokens, model_width)
    hidden_pre = jnp.dot(normed_flat, fc_one, preferred_element_type=jnp.float32) + bias_fc
    active, pull_gate = jax.vjp(smooth_gate, hidden_pre)
    active_flat = active.astype(jnp.bfloat16)
    upstream = cotangent.reshape(tokens, model_width)
    term_two = jnp.einsum("tf,td->fd", active_flat, upstream, preferred_element_type=jnp.float32)
    part_two = lax.psum_scatter(
        term_two.astype(jnp.bfloat16), everyone, scatter_dimension=0, tiled=True
    )
    grad_active = jnp.einsum("td,fd->tf", upstream, fc_two, preferred_element_type=jnp.float32)
    grad_hidden = pull_gate(grad_active)[0]
    grad_hidden_flat = grad_hidden.astype(jnp.bfloat16)
    term_one = jnp.einsum(
        "tf,td->fd", grad_hidden_flat, normed_flat, preferred_element_type=jnp.float32
    )
    part_one = lax.psum_scatter(
        term_one.astype(jnp.bfloat16), everyone, scatter_dimension=0, tiled=True
    )
    grad_normed_two = jnp.einsum(
        "tf,df->td", grad_hidden_flat, fc_one, preferred_element_type=jnp.float32
    )
    grad_mixed_norm, grad_gain_two = pull_two(grad_normed_two.reshape(mixed_field.shape))
    grad_mixed = cotangent.astype(jnp.float32) + grad_mixed_norm
    grad_spectrum = to_modes(grad_mixed, zonal_back, merid, blocks, jnp.bfloat16)
    pulled = pull_mix(grad_spectrum)
    grad_normed = grad_mixed + from_modes(
        pulled[0], zonal, merid, samples, model_width, jnp.bfloat16
    )
    grad_base, grad_gain_one = pull_one(grad_normed)
    grad_input = grad_mixed + grad_base
    bias_sum = jnp.sum(grad_hidden, axis=0)
    out_sum = jnp.sum(cotangent, axis=(0, 1, 2), dtype=jnp.float32)
    totals = lax.psum(
        (
            grad_gain_one,
            grad_gain_two,
            pulled[1],
            pulled[2],
            pulled[3],
            pulled[4],
            bias_sum,
            out_sum,
        ),
        everyone,
    )
    grad_scale = 1.0 / math.sqrt(samples * lax.axis_size("dp") * lat_total * lon_cells)
    return (
        grad_input,
        (part_one.astype(jnp.float32) * grad_scale).T,
        part_two.astype(jnp.float32) * grad_scale,
        totals[6] * grad_scale,
        totals[7] * grad_scale,
        totals[0] * grad_scale,
        totals[1] * grad_scale,
        totals[2] * grad_scale,
        totals[3] * grad_scale,
        totals[4] * grad_scale,
        totals[5] * grad_scale,
    )


def solution(mesh):
    placed = (
        P("space", None, "dp", None),
        P(None, "space"),
        P(),
        P(),
        P(),
        P(),
        P(),
        P(),
        P(),
        P(),
        P(),
        P("dp", "space", None, None),
    )
    return jax.shard_map(
        local,
        mesh=mesh,
        in_specs=placed,
        out_specs=(
            P("dp", "space", None, None),
            P(None, ("dp", "space")),
            P(("dp", "space"), None),
            P(),
            P(),
            P(),
            P(),
            P(),
            P(),
            P(),
            P(),
        ),
        check_vma=False,
    )
```

```python
import functools
import math

import jax
import jax.numpy as jnp
import numpy as np
from jax import lax
from jax.experimental import pallas as pl
from jax.experimental.pallas import tpu as pltpu
from jax.sharding import PartitionSpec as P

KW = 64


epsilon = 1e-05
high = lax.Precision.HIGH
everyone = ("dp", "space")


def layer_norm(values, gain_vector):
    centred = values - jnp.mean(values, axis=-1, keepdims=True)
    spread = jnp.mean(centred * centred, axis=-1, keepdims=True)
    return centred * lax.rsqrt(spread + epsilon) * gain_vector


def smooth_gate(values):
    return jax.nn.gelu(values, approximate=True)


def complex_blocks(weights):
    top = jnp.concatenate((weights[0], weights[1]), axis=2)
    bottom = jnp.concatenate((-weights[1], weights[0]), axis=2)
    return jnp.concatenate((top, bottom), axis=1)


def complex_bias(biases, blocks):
    return biases.reshape(2, blocks, 1, -1).transpose(1, 2, 0, 3).reshape(blocks, 1, -1)


def block_dot(values, weights):
    return jnp.einsum("nri,nio->nro", values, weights, precision=high)


def spectral_mlp(spectrum, spec_one, bias_one, spec_two, bias_two):
    blocks = spec_one.shape[1]
    inner = block_dot(spectrum, complex_blocks(spec_one)) + complex_bias(bias_one, blocks)
    return block_dot(smooth_gate(inner), complex_blocks(spec_two)) + complex_bias(bias_two, blocks)


def zonal_tables(length, ranks):
    positions = np.arange(length)[:, None]
    frequency = np.arange(KW)[None, :]
    angles = (positions * frequency % length) * (2.0 * math.pi / length)
    table = np.stack((np.cos(angles), -np.sin(angles))) / math.sqrt(length)
    doubled = table * np.where(frequency == 0, 1.0, 2.0)
    shaped = [
        item.reshape(2, length, ranks, KW // ranks).transpose(1, 2, 0, 3).astype(np.float32)
        for item in (table, doubled)
    ]
    return shaped


def meridian_table(length, ranks):
    positions = np.arange(length)
    angles = (positions[:, None] * positions[None, :] % length) * (2.0 * math.pi / length)
    cosine = np.cos(angles) / math.sqrt(length)
    sine = np.sin(angles) / math.sqrt(length)
    table = np.stack((np.stack((cosine, -sine), -1), np.stack((sine, cosine), -1)), 1)
    return table.reshape(ranks, length // ranks, 2, length, 2).astype(np.float32)


def swap(pieces):
    return lax.all_to_all(pieces, "space", split_axis=0, concat_axis=0, tiled=True)


def to_modes(field, zonal, merid, blocks, carried):
    pieces = jnp.einsum("brwd,wscm->sbrcmd", field, zonal, precision=high)
    modes = swap(pieces.astype(carried)).astype(jnp.float32)
    spectrum = jnp.einsum("lbrcmd,lrcke->bmked", modes, merid, precision=high)
    rows = math.prod(spectrum.shape[:3])
    split = spectrum.reshape(rows, 2, blocks, -1)
    return split.transpose(2, 0, 1, 3).reshape(blocks, rows, -1)


def from_modes(spectrum, zonal, merid, samples, width, carried):
    blocks, rows = spectrum.shape[:2]
    length = merid.shape[3]
    split = spectrum.reshape(blocks, rows, 2, -1).transpose(1, 2, 0, 3)
    shaped = split.reshape(samples, rows // (samples * length), length, 2, width)
    pieces = jnp.einsum("bmked,lrcke->lbrcmd", shaped, merid, precision=high)
    modes = swap(pieces.astype(carried)).astype(jnp.float32)
    return jnp.einsum("sbrcmd,wscm->brwd", modes, zonal, precision=high)


def total_kernel(ranks, space_ranks, scale, terms, result, landed, kept, gathered, *sems):
    me = lax.axis_index("dp") * space_ranks + lax.axis_index("space")
    send_term, recv_term, send_sum, recv_sum = sems

    def place(peer):
        return (peer // space_ranks, lax.rem(peer, space_ranks))

    def term_copy(step):
        peer = lax.rem(me + step, ranks)
        return pltpu.make_async_remote_copy(
            src_ref=terms.at[peer],
            dst_ref=landed.at[me],
            send_sem=send_term.at[step],
            recv_sem=recv_term.at[step],
            device_id=place(peer),
            device_id_type=pl.DeviceIdType.MESH,
        )

    def sum_copy(step):
        peer = lax.rem(me + step, ranks)
        return pltpu.make_async_remote_copy(
            src_ref=kept,
            dst_ref=gathered.at[me],
            send_sem=send_sum.at[step],
            recv_sem=recv_sum.at[step],
            device_id=place(peer),
            device_id_type=pl.DeviceIdType.MESH,
        )

    barrier = pltpu.get_barrier_semaphore()

    def greet(step, carry):
        pl.semaphore_signal(
            barrier,
            inc=1,
            device_id=place(lax.rem(me + step, ranks)),
            device_id_type=pl.DeviceIdType.MESH,
        )
        return carry

    def send_terms(step, carry):
        term_copy(step).start()
        return carry

    def add_term(step, carry):
        term_copy(step).wait_recv()
        return carry + landed[lax.rem(me + ranks - step, ranks)]

    def send_sums(step, carry):
        sum_copy(step).start()
        return carry

    def finish(step, carry):
        term_copy(step).wait_send()
        sum_copy(step).wait()
        return carry

    lax.fori_loop(1, ranks, greet, 0)
    pl.semaphore_wait(barrier, ranks - 1)
    lax.fori_loop(1, ranks, send_terms, 0)
    total = lax.fori_loop(1, ranks, add_term, terms[me]) * scale
    kept[...] = total
    lax.fori_loop(1, ranks, send_sums, 0)
    lax.fori_loop(1, ranks, finish, 0)
    gathered[me] = total
    result[...] = gathered[...]


def scaled_totals(parts, ranks, space_ranks, scale):
    flat = jnp.concatenate([part.reshape(-1) for part in parts])
    block = 8 * 128
    rows = -(-flat.size // (ranks * block)) * 8
    padded = jnp.pad(flat, (0, ranks * rows * 128 - flat.size)).reshape(ranks, rows, 128)
    vmem = pl.BlockSpec(memory_space=pltpu.VMEM)
    summed = pl.pallas_call(
        functools.partial(total_kernel, ranks, space_ranks, scale),
        out_shape=jax.ShapeDtypeStruct(padded.shape, jnp.float32),
        in_specs=[vmem],
        out_specs=vmem,
        scratch_shapes=[
            pltpu.VMEM(padded.shape, jnp.float32),
            pltpu.VMEM(padded.shape[1:], jnp.float32),
            pltpu.VMEM(padded.shape, jnp.float32),
        ]
        + [pltpu.SemaphoreType.DMA((ranks,))] * 4,
        compiler_params=pltpu.CompilerParams(collective_id=0, has_side_effects=True),
    )(padded)
    flat_sum = summed.reshape(-1)
    found, at = [], 0
    for part in parts:
        found.append(lax.slice(flat_sum, (at,), (at + part.size,)).reshape(part.shape))
        at += part.size
    return found


def scattered(term, dp_ranks, space_ranks):
    width = term.shape[-1]
    lanes = term.reshape(dp_ranks, space_ranks, -1, width).transpose(1, 0, 2, 3)
    rows = lanes.reshape(term.shape).astype(jnp.bfloat16)
    return rows


def paired(part, dp_ranks):
    wide = part.astype(jnp.float32).reshape(dp_ranks, -1, part.shape[-1])
    return wide


def local(
    stash,
    piece_map,
    gain_one,
    spec_one,
    bias_one,
    spec_two,
    bias_two,
    gain_two,
    fc_one,
    bias_fc,
    fc_two,
    cotangent,
):
    samples, lat_rows, lon_cells, model_width = cotangent.shape
    space_ranks = lax.axis_size("space")
    dp_ranks = lax.axis_size("dp")
    lat_total = lat_rows * space_ranks
    tokens = samples * lat_rows * lon_cells
    blocks = spec_one.shape[1]
    arrived = lax.all_to_all(stash, "space", split_axis=1, concat_axis=0, tiled=True)
    ordering = jnp.argsort(piece_map[:, 0])
    placed = jnp.take(arrived[:, 0], ordering, axis=0)
    inputs = jnp.transpose(placed, (1, 0, 2)).reshape(samples, lat_rows, lon_cells, model_width)
    base_field = inputs.astype(jnp.float32)
    zonal, zonal_back = zonal_tables(lon_cells, space_ranks)
    merid = meridian_table(lat_total, space_ranks)
    normed, pull_one = jax.vjp(layer_norm, base_field, gain_one)
    spectrum = to_modes(normed, zonal, merid, blocks, jnp.float32)
    mixed_spec, pull_mix = jax.vjp(spectral_mlp, spectrum, spec_one, bias_one, spec_two, bias_two)
    spatial = from_modes(
        mixed_spec, zonal_back, merid, samples, model_width, jnp.float32
    )
    mixed_field = base_field + normed + spatial
    normed_two, pull_two = jax.vjp(layer_norm, mixed_field, gain_two)
    normed_flat = normed_two.astype(jnp.bfloat16).reshape(tokens, model_width)
    hidden_pre = jnp.dot(normed_flat, fc_one, preferred_element_type=jnp.float32) + bias_fc
    active, pull_gate = jax.vjp(smooth_gate, hidden_pre)
    active_flat = active.astype(jnp.bfloat16)
    upstream = cotangent.reshape(tokens, model_width)
    term_two = jnp.einsum("tf,td->fd", active_flat, upstream, preferred_element_type=jnp.float32)
    grad_active = jnp.einsum("td,fd->tf", upstream, fc_two, preferred_element_type=jnp.float32)
    grad_hidden = pull_gate(grad_active)[0]
    grad_hidden_flat = grad_hidden.astype(jnp.bfloat16)
    term_one = jnp.einsum(
        "tf,td->fd", grad_hidden_flat, normed_flat, preferred_element_type=jnp.float32
    )
    grad_normed_two = jnp.einsum(
        "tf,df->td", grad_hidden_flat, fc_one, preferred_element_type=jnp.float32
    )
    rows_one = scattered(term_one, dp_ranks, space_ranks)
    rows_two = scattered(term_two, dp_ranks, space_ranks)
    grad_normed_two, rows_one, rows_two = lax.optimization_barrier(
        (grad_normed_two, rows_one, rows_two)
    )
    part_two = lax.psum_scatter(rows_two, "space", scatter_dimension=0, tiled=True)
    part_one = lax.psum_scatter(rows_one, "space", scatter_dimension=0, tiled=True)
    grad_mixed_norm, grad_gain_two = pull_two(grad_normed_two.reshape(mixed_field.shape))
    grad_mixed = cotangent.astype(jnp.float32) + grad_mixed_norm
    grad_spectrum = to_modes(grad_mixed, zonal_back, merid, blocks, jnp.bfloat16)
    pulled = pull_mix(grad_spectrum)
    grad_normed = grad_mixed + from_modes(
        pulled[0], zonal, merid, samples, model_width, jnp.bfloat16
    )
    grad_base, grad_gain_one = pull_one(grad_normed)
    grad_input = grad_mixed + grad_base
    bias_sum = jnp.sum(grad_hidden, axis=0)
    out_sum = jnp.sum(cotangent, axis=(0, 1, 2), dtype=jnp.float32)
    grad_scale = 1.0 / math.sqrt(samples * dp_ranks * lat_total * lon_cells)
    totals = scaled_totals(
        (
            pulled[1],
            pulled[3],
            pulled[2],
            pulled[4],
            grad_gain_one,
            grad_gain_two,
            bias_sum,
            out_sum,
        ),
        dp_ranks * space_ranks,
        space_ranks,
        grad_scale,
    )
    both = jnp.stack((paired(part_one, dp_ranks), paired(part_two, dp_ranks)), axis=1)
    halves = lax.all_to_all(both, "dp", split_axis=0, concat_axis=0, tiled=True)
    summed = jnp.sum(halves, axis=0) * grad_scale
    return (
        grad_input,
        summed[0].T,
        summed[1],
        totals[6],
        totals[7],
        totals[4],
        totals[5],
        totals[0],
        totals[2],
        totals[1],
        totals[3],
    )


def solution(mesh):
    placed = (
        P("space", None, "dp", None),
        P(None, "space"),
        P(),
        P(),
        P(),
        P(),
        P(),
        P(),
        P(),
        P(),
        P(),
        P("dp", "space", None, None),
    )
    return jax.shard_map(
        local,
        mesh=mesh,
        in_specs=placed,
        out_specs=(
            P("dp", "space", None, None),
            P(None, ("dp", "space")),
            P(("dp", "space"), None),
            P(),
            P(),
            P(),
            P(),
            P(),
            P(),
            P(),
            P(),
        ),
        check_vma=False,
    )
```
